32 devices in a mesh: exp: 8 (over z, x), seq: 4 (over y, core).
Axes of the slice: x: 2, y: 2, z: 4, core: 2. Of those that a mesh axis runs over, the one named last changes fastest.
Arguments:
- out_grad: bfloat16 [4096, 4096], P(('exp', 'seq')), may hold values from -1.5 to 1.5
- chosen: int32 [8, 1024], P('exp'), may hold values from 0 to 4095, as said below
- scores: float32 [8, 1024], P('exp'), may hold values from 0.05 to 1
- saved_pre: bfloat16 [8, 1024, 2, 1536], P('exp', None, None, 'seq'), may hold values from -6 to 6
- gate_up: bfloat16 [8, 4096, 2, 1536], P('exp', None, None, 'seq'), may hold values from -0.09375 to 0.09375
- down: bfloat16 [8, 1536, 4096], P('exp', 'seq'), may hold values from -0.15625 to 0.15625
Outputs:
- in_grad: bfloat16 [4096, 4096], P(('exp', 'seq'))
- score_grad: float32 [8, 1024], P('exp')
The draws below stay inside these ranges and needn't reach their ends.
Inputs may be any that keep to these rules, and one draw needn't show every extreme that they name: `chosen`: each row lists 1024 different tokens. At most 144 of one row's tokens lie in one block of 512 consecutive tokens (the tokens of one index of exp), and every row has exactly 144 in some block.
All inputs are finite; a program needn't handle non-finite values.
Results may differ from the reference program's by a relative error of at most 0.012.
Values may be sent and summed in bfloat16 or wider, within the bound.
A program may use at most 128 MiB of HBM per device.

```python
import math
import jax
import jax.numpy as jnp
from jax import lax

D = 4096
FF = 1536
EXPERTS = 8
TOKENS = 4096
CAP = 1024
GROUP_TOK = 512
GROUP_MOST = 144
N_SEQ = 4


def draw_chosen(key, part):
    base_key = jax.random.fold_in(key, 11)
    key_groups, key_tokens, key_shuffle = jax.random.split(base_key, 3)
    mean_quota = CAP // EXPERTS
    pattern = jnp.array([9, 9, 8, 6], jnp.int32) * mean_quota // 8
    group_scores = jax.random.randint(key_groups, (EXPERTS, EXPERTS), 0, 65536) * EXPERTS + jnp.arange(EXPERTS, dtype=jnp.int32)[None, :]
    group_order = jnp.argsort(group_scores, axis=1)
    group_place = jnp.argsort(group_order, axis=1).astype(jnp.int32)
    group_quota = pattern[group_place % 4]
    token_scores = jax.random.randint(key_tokens, (EXPERTS, EXPERTS, GROUP_TOK), 0, 16384) * GROUP_TOK + jnp.arange(GROUP_TOK, dtype=jnp.int32)[None, None, :]
    candidates = jnp.argsort(token_scores, axis=2)[:, :, :GROUP_MOST].astype(jnp.int32)
    candidates = candidates + (jnp.arange(EXPERTS, dtype=jnp.int32) * GROUP_TOK)[None, :, None]
    usable = (jnp.arange(GROUP_MOST, dtype=jnp.int32)[None, None, :] < group_quota[:, :, None]).astype(jnp.int32)
    flat_tokens = candidates.reshape(EXPERTS, EXPERTS * GROUP_MOST)
    flat_usable = usable.reshape(EXPERTS, EXPERTS * GROUP_MOST)
    shuffle_scores = jax.random.randint(key_shuffle, (EXPERTS, EXPERTS * GROUP_MOST), 0, 32768) * (EXPERTS * GROUP_MOST) + jnp.arange(EXPERTS * GROUP_MOST, dtype=jnp.int32)[None, :]
    shuffle = jnp.argsort(shuffle_scores, axis=1)
    flat_tokens = jnp.take_along_axis(flat_tokens, shuffle, axis=1)
    flat_usable = jnp.take_along_axis(flat_usable, shuffle, axis=1)
    keep_order = jnp.argsort(1 - flat_usable, axis=1, stable=True)[:, :CAP]
    return jnp.take_along_axis(flat_tokens, keep_order, axis=1).astype(jnp.int32)


def block_levels(own_key, dims, pieces, least, top_value):
    def one(position, blocks):
        steps = jax.random.uniform(jax.random.fold_in(jax.random.fold_in(own_key, 6), position), (blocks,), jnp.float32, least / len(pieces), top_value / len(pieces))
        return jnp.repeat(jnp.exp(steps), dims[position] // blocks).reshape((-1,) + (1,) * (len(dims) - position - 1))

    factor_of = one(*pieces[0])
    for cut in pieces[1:]:
        factor_of = factor_of * one(*cut)
    return factor_of


def bell_draw(rng, extent, deviation, bound, cuts=(), kind=jnp.bfloat16):
    loudness = block_levels(rng, extent, cuts, -0.22, 0.18) if cuts else 1.0
    entries = jax.random.normal(rng, extent, jnp.float32) * deviation * loudness
    return jnp.minimum(jnp.maximum(entries, -bound), bound).astype(kind)


def setup_inputs(seed: int = 0) -> dict:
    key_list = jax.random.split(jax.random.key(seed), 7)
    return {
        "out_grad": bell_draw(key_list[0], (TOKENS, D), 0.25, 1.5, ((0, 32),)),
        "chosen": draw_chosen(jax.random.fold_in(key_list[6], 71), 0),
        "scores": jnp.clip(jnp.exp(math.log(1.0) - 2.9957323 * jax.random.uniform(key_list[2], (EXPERTS, CAP), jnp.float32) ** block_levels(key_list[2], (EXPERTS, CAP), ((0, 8),), -0.2, 0.2)), 0.05, 1.0),
        "saved_pre": bell_draw(key_list[3], (EXPERTS, CAP, 2, FF), 1.0, 6.0, ((0, 8), (3, 4))),
        "gate_up": bell_draw(key_list[4], (EXPERTS, D, 2, FF), D ** -0.5, 0.09375, ((0, 8), (3, 4))),
        "down": bell_draw(key_list[5], (EXPERTS, FF, D), FF ** -0.5, 0.15625, ((0, 8), (1, 4))),
    }


def reference(out_grad, chosen, scores, saved_pre, gate_up, down):
    quarter = FF // N_SEQ

    def per_expert(totals, expert_data):
        token_ids, weight, pre, mixing, down_e = expert_data
        dy_rows = out_grad[token_ids]
        back_grad = jnp.dot(dy_rows, down_e.T, preferred_element_type=jnp.float32)
        gate_pre = pre[:, 0].astype(jnp.float32)
        up_pre = pre[:, 1].astype(jnp.float32)
        sigmoid_gate = jax.nn.sigmoid(gate_pre)
        activated = gate_pre * sigmoid_gate
        hidden = (activated * up_pre).astype(jnp.bfloat16)
        hidden = lax.optimization_barrier(hidden)
        score_part = jnp.sum(hidden.astype(jnp.float32) * back_grad, axis=1)
        scaled = weight[:, None] * back_grad
        d_gate = scaled * up_pre * sigmoid_gate * (1.0 + gate_pre * (1.0 - sigmoid_gate))
        d_up = scaled * activated
        d_both = jnp.stack([d_gate, d_up], axis=1).astype(jnp.bfloat16)
        left = d_both.reshape(CAP, 2, N_SEQ, quarter).astype(jnp.float32)
        right = mixing.reshape(D, 2, N_SEQ, quarter).astype(jnp.float32)
        partial_value = jnp.einsum('ckqh,dkqh->qcd', left, right).astype(jnp.bfloat16)
        partial_value = lax.optimization_barrier(partial_value)
        summed = jnp.sum(partial_value.astype(jnp.float32), axis=0)
        totals = totals.at[token_ids].add(summed)
        return totals, score_part

    start = jnp.zeros((TOKENS, D), jnp.float32)
    totals, score_grad = lax.scan(per_expert, start, (chosen, scores, saved_pre, gate_up, down))
    return totals.astype(jnp.bfloat16), score_grad
```

```python
import functools

import jax
import jax.numpy as jnp
from jax import lax
from jax.experimental import pallas as pl
from jax.experimental.pallas import tpu as pltpu
from jax.sharding import PartitionSpec as P

MESH = pl.DeviceIdType.MESH
ANY = pl.BlockSpec(memory_space=pl.ANY)
VMEM = pl.BlockSpec(memory_space=pltpu.VMEM)


def flip(index, bits):
    out, step = index, 1
    while bits >= step:
        if bits & step:
            out = out + step * (1 - 2 * ((index // step) % 2))
        step *= 2
    return out


def greet(peers):
    barrier = pltpu.get_barrier_semaphore()
    for p in peers:
        pl.semaphore_signal(barrier, inc=1, device_id=p, device_id_type=MESH)
    pl.semaphore_wait(barrier, len(peers))


def remote(src, dst, send, recv, to):
    return pltpu.make_async_remote_copy(
        src_ref=src, dst_ref=dst, send_sem=send, recv_sem=recv, device_id=to, device_id_type=MESH
    )


def columns(quarter, width):
    return pl.ds(pl.multiple_of(quarter * width, 128), width)


def exchange_kernel(n_exp, n_seq, chosen, grad, ids, group, send_i, recv_i, send_g, recv_g, local):
    g, s = lax.axis_index("exp"), lax.axis_index("seq")
    width = grad.shape[1] // n_seq
    greet([(flip(g, k), s) for k in range(1, n_exp)] + [(g, flip(s, k)) for k in range(1, n_seq)])
    copies = []
    for k in range(1, n_exp):
        copies.append(remote(chosen, ids.at[g], send_i.at[k], recv_i.at[k], (flip(g, k), s)))
        copies[-1].start()
    for k in range(n_seq - 1, 0, -1):
        t = flip(s, k)
        copies.append(
            remote(grad.at[:, columns(t, width)], group.at[s], send_g.at[k], recv_g.at[k], (g, t))
        )
        copies[-1].start()
    own_ids = pltpu.make_async_copy(chosen, ids.at[g], local.at[0])
    own_grad = pltpu.make_async_copy(grad.at[:, columns(s, width)], group.at[s], local.at[1])
    own_ids.start()
    own_grad.start()
    for c in copies:
        c.wait()
    own_ids.wait()
    own_grad.wait()


def exchange(n_exp, n_seq, chosen, grad):
    rows, width = grad.shape[0], grad.shape[1] // n_seq
    dma = pltpu.SemaphoreType.DMA
    return pl.pallas_call(
        functools.partial(exchange_kernel, n_exp, n_seq),
        out_shape=(
            jax.ShapeDtypeStruct((n_exp,) + chosen.shape, chosen.dtype),
            jax.ShapeDtypeStruct((n_seq, rows, width), grad.dtype),
        ),
        in_specs=[VMEM, VMEM],
        out_specs=(VMEM, VMEM),
        scratch_shapes=[dma((n_exp,)), dma((n_exp,)), dma((n_seq,)), dma((n_seq,)), dma((2,))],
        compiler_params=pltpu.CompilerParams(collective_id=0, has_side_effects=True),
    )(chosen, grad)


def dispatch_kernel(n_exp, out, fetched, s0, r0, sa, ra, sb, rb, sc, rc, local):
    g, s = lax.axis_index("exp"), lax.axis_index("seq")
    width = out.shape[2]
    across, beside = (g, flip(s, 2)), (g, flip(s, 1))
    own, theirs = columns(s, width), columns(flip(s, 2), width)
    greet([(flip(g, k), s) for k in range(1, n_exp)] + [across, beside])
    first = pltpu.make_async_copy(out.at[g], fetched.at[g, :, own], local)
    first.start()
    half = n_exp // 2
    order = []
    for k in range(half):
        order.append(half + k)
        if k:
            order.append(k)
    sends = {}
    for k in order:
        e = flip(g, k)
        sends[k] = remote(out.at[e], fetched.at[g, :, own], s0.at[k], r0.at[k], (e, s))
        sends[k].start()
    crossed, done = [], []
    for k in range(n_exp):
        block = fetched.at[flip(g, k)]
        if k:
            sends[k].wait_recv()
        else:
            first.wait()
        c = remote(block.at[:, own], block.at[:, own], sa.at[k], ra.at[k], across)
        c.start()
        crossed.append(c)
        d = remote(block.at[:, own], block.at[:, own], sb.at[k], rb.at[k], beside)
        d.start()
        done.append(d)
    for k in range(n_exp):
        block = fetched.at[flip(g, k)]
        crossed[k].wait_recv()
        d = remote(block.at[:, theirs], block.at[:, theirs], sc.at[k], rc.at[k], beside)
        d.start()
        done.append(d)
    for k in order:
        sends[k].wait_send()
    for c in crossed:
        c.wait_send()
    for d in done:
        d.wait()


def dispatch(n_exp, n_seq, out):
    rows, width = out.shape[1:]
    dma = pltpu.SemaphoreType.DMA
    return pl.pallas_call(
        functools.partial(dispatch_kernel, n_exp),
        out_shape=jax.ShapeDtypeStruct((n_exp, rows, n_seq * width), out.dtype),
        in_specs=[ANY],
        out_specs=ANY,
        scratch_shapes=[dma((n_exp,))] * 8 + [dma],
        compiler_params=pltpu.CompilerParams(collective_id=1, has_side_effects=True),
    )(out)


def combine_kernel(n_exp, part, arrived, near, sum1, far, sum2, s1, r1, s2, r2, s3, r3, local):
    g, s = lax.axis_index("exp"), lax.axis_index("seq")
    width = arrived.shape[2]
    across, beside = (g, flip(s, 2)), (g, flip(s, 1))
    own, theirs = columns(s, width), columns(flip(s, 2), width)
    greet([(flip(g, k), s) for k in range(1, n_exp)] + [across, beside])
    half = n_exp // 2
    order = list(range(half, n_exp)) + list(range(1, half)) + [0]
    pairs = {}
    for k in order:
        e = flip(g, k)
        pairs[k] = [
            remote(
                part.at[e, :, columns(flip(s, bits), width)],
                near.at[e, i],
                s1.at[k, i],
                r1.at[k, i],
                beside,
            )
            for i, bits in enumerate((3, 1))
        ]
        for c in pairs[k]:
            c.start()
    middle, last = {}, {}
    for k in order:
        e = flip(g, k)
        pairs[k][0].wait_recv()
        both = part[e, :, theirs].astype(jnp.float32) + near[e, 0].astype(jnp.float32)
        sum1[e] = both.astype(jnp.bfloat16)
        middle[k] = remote(sum1.at[e], far.at[e], s2.at[k], r2.at[k], across)
        middle[k].start()
    for k in order:
        e = flip(g, k)
        pairs[k][1].wait_recv()
        middle[k].wait_recv()
        total = part[e, :, own].astype(jnp.float32) + near[e, 1].astype(jnp.float32)
        total = total + far[e].astype(jnp.float32)
        sum2[e] = total.astype(jnp.bfloat16)
        if k:
            last[k] = remote(sum2.at[e], arrived.at[g], s3.at[k], r3.at[k], (e, s))
        else:
            last[k] = pltpu.make_async_copy(sum2.at[e], arrived.at[g], local)
        last[k].start()
    for k in order:
        for c in pairs[k]:
            c.wait_send()
        middle[k].wait_send()
        last[k].wait()


def combine(n_exp, n_seq, part):
    rows, width = part.shape[1], part.shape[2] // n_seq
    dma = pltpu.SemaphoreType.DMA
    block = pltpu.VMEM((n_exp, rows, width), part.dtype)
    return pl.pallas_call(
        functools.partial(combine_kernel, n_exp),
        out_shape=jax.ShapeDtypeStruct((n_exp, rows, width), part.dtype),
        in_specs=[VMEM],
        out_specs=VMEM,
        scratch_shapes=[pltpu.VMEM((n_exp, 2, rows, width), part.dtype), block, block, block]
        + [dma((n_exp, 2))] * 2
        + [dma((n_exp,))] * 4
        + [dma],
        compiler_params=pltpu.CompilerParams(
            collective_id=2, has_side_effects=True, vmem_limit_bytes=48 * 2**20
        ),
    )(part)


def regroup_kernel(n_seq, totals, out, send, recv, local):
    g, s = lax.axis_index("exp"), lax.axis_index("seq")
    width = totals.shape[2]
    own = columns(s, width)
    greet([(g, flip(s, k)) for k in range(1, n_seq)])
    copies = []
    for k in range(n_seq - 1, 0, -1):
        t = flip(s, k)
        copies.append(remote(totals.at[t], out.at[:, own], send.at[k], recv.at[k], (g, t)))
        copies[-1].start()
    mine = pltpu.make_async_copy(totals.at[s], out.at[:, own], local)
    mine.start()
    for c in copies:
        c.wait()
    mine.wait()


def regroup(n_seq, totals):
    rows, width = totals.shape[1:]
    dma = pltpu.SemaphoreType.DMA
    return pl.pallas_call(
        functools.partial(regroup_kernel, n_seq),
        out_shape=jax.ShapeDtypeStruct((rows, n_seq * width), totals.dtype),
        in_specs=[VMEM],
        out_specs=VMEM,
        scratch_shapes=[dma((n_seq,)), dma((n_seq,)), dma],
        compiler_params=pltpu.CompilerParams(collective_id=3, has_side_effects=True),
    )(totals)


def local(out_grad, chosen, scores, saved_pre, gate_up, down):
    n_exp = lax.axis_size("exp")
    n_seq = lax.axis_size("seq")
    capacity = chosen.shape[1]
    slot_most = 9 * capacity // (8 * n_exp)
    tok_count, model_width = out_grad.shape
    width = model_width // n_seq
    group_tok = tok_count * n_seq
    pad_rows = n_exp * slot_most
    hidden_part = gate_up.shape[3]
    group_index = lax.axis_index("exp")

    own_ids = chosen[0]
    owner_group = own_ids // group_tok
    owner_hits = (owner_group[None, :] == jnp.arange(n_exp, dtype=jnp.int32)[:, None]).astype(
        jnp.int32
    )
    slot_order = jnp.sum(jnp.cumsum(owner_hits, axis=1) * owner_hits, axis=0) - 1
    position = owner_group * slot_most + slot_order
    place = position[None, :] == jnp.arange(pad_rows, dtype=jnp.int32)[:, None]
    weight_padded = jnp.sum(jnp.where(place, scores[0][None, :], 0.0), axis=1)
    place_one = place.astype(jnp.bfloat16)

    def padded(x):
        return jnp.dot(place_one, x, preferred_element_type=jnp.float32)

    gate_pre = padded(saved_pre[0, :, 0])
    up_pre = padded(saved_pre[0, :, 1])
    mixing = gate_up[0].reshape(model_width, 2 * hidden_part)

    ids, group = exchange(n_exp, n_seq, chosen.reshape(capacity // 128, 128), out_grad)
    local_ids = ids.reshape(n_exp, capacity) - group_index * group_tok
    inside = (local_ids >= 0) & (local_ids < group_tok)
    slot_rank = jnp.cumsum(inside.astype(jnp.int32), axis=1) - 1
    slot_ids = jnp.arange(slot_most, dtype=jnp.int32)
    picked = inside[:, None, :] & (slot_rank[:, None, :] == slot_ids[None, :, None])
    source = jnp.sum(jnp.where(picked, local_ids[:, None, :] + 1, 0), axis=2).reshape(pad_rows) - 1
    tokens = jnp.arange(group_tok, dtype=jnp.int32)
    take = (source[:, None] == tokens[None, :]).astype(jnp.bfloat16)
    outgoing = jnp.dot(
        take, group.reshape(group_tok, width), preferred_element_type=jnp.float32
    ).astype(jnp.bfloat16)
    fetched = dispatch(n_exp, n_seq, outgoing.reshape(n_exp, slot_most, width))
    fetched = fetched.reshape(pad_rows, model_width)

    back_grad = lax.dot_general(
        fetched, down[0], (((1,), (1,)), ((), ())), preferred_element_type=jnp.float32
    )
    sigmoid_gate = jax.nn.sigmoid(gate_pre)
    activated = gate_pre * sigmoid_gate
    hidden = (activated * up_pre).astype(jnp.bfloat16)
    hidden = lax.optimization_barrier(hidden)
    score_part = jnp.sum(hidden.astype(jnp.float32) * back_grad, axis=1)
    scaled = weight_padded[:, None] * back_grad
    d_gate = scaled * up_pre * sigmoid_gate * (1.0 + gate_pre * (1.0 - sigmoid_gate))
    d_up = scaled * activated
    d_both = jnp.concatenate([d_gate, d_up], axis=1).astype(jnp.bfloat16)
    partial_value = lax.dot_general(
        d_both, mixing, (((1,), (1,)), ((), ())), preferred_element_type=jnp.float32
    ).astype(jnp.bfloat16)
    score_slots = jnp.sum(jnp.where(place, score_part[:, None], 0.0), axis=0)
    score_grad = lax.psum(score_slots, "seq")[None, :]

    arrived = combine(n_exp, n_seq, partial_value.reshape(n_exp, slot_most, model_width))
    totals = lax.dot_general(
        take,
        arrived.reshape(pad_rows, width),
        (((0,), (0,)), ((), ())),
        preferred_element_type=jnp.float32,
    ).astype(jnp.bfloat16)
    summed = regroup(n_seq, totals.reshape(n_seq, tok_count, width))
    return (summed, score_grad)


def solution(mesh):
    return jax.shard_map(
        local,
        mesh=mesh,
        in_specs=(
            P(("exp", "seq"), None),
            P("exp", None),
            P("exp", None),
            P("exp", None, None, "seq"),
            P("exp", None, None, "seq"),
            P("exp", "seq", None),
        ),
        out_specs=(P(("exp", "seq"), None), P("exp", None)),
        check_vma=False,
    )
```

```python
import functools

import jax
import jax.numpy as jnp
from jax import lax
from jax.experimental import pallas as pl
from jax.experimental.pallas import tpu as pltpu
from jax.sharding import PartitionSpec as P

MESH = pl.DeviceIdType.MESH
ANY = pl.BlockSpec(memory_space=pl.ANY)
VMEM = pl.BlockSpec(memory_space=pltpu.VMEM)


def flip(index, bits):
    out, step = index, 1
    while bits >= step:
        if bits & step:
            out = out + step * (1 - 2 * ((index // step) % 2))
        step *= 2
    return out


def greet(peers):
    barrier = pltpu.get_barrier_semaphore()
    for p in peers:
        pl.semaphore_signal(barrier, inc=1, device_id=p, device_id_type=MESH)
    pl.semaphore_wait(barrier, len(peers))


def remote(src, dst, send, recv, to):
    return pltpu.make_async_remote_copy(
        src_ref=src, dst_ref=dst, send_sem=send, recv_sem=recv, device_id=to, device_id_type=MESH
    )


def columns(quarter, width):
    return pl.ds(pl.multiple_of(quarter * width, 128), width)


def exchange_kernel(n_exp, n_seq, chosen, grad, ids, group, send_i, recv_i, send_g, recv_g, local):
    g, s = lax.axis_index("exp"), lax.axis_index("seq")
    width = grad.shape[1] // n_seq
    greet([(flip(g, k), s) for k in range(1, n_exp)] + [(g, flip(s, k)) for k in range(1, n_seq)])
    copies = []
    for k in range(1, n_exp):
        copies.append(remote(chosen, ids.at[g], send_i.at[k], recv_i.at[k], (flip(g, k), s)))
        copies[-1].start()
    for k in range(n_seq - 1, 0, -1):
        t = flip(s, k)
        copies.append(
            remote(grad.at[:, columns(t, width)], group.at[s], send_g.at[k], recv_g.at[k], (g, t))
        )
        copies[-1].start()
    own_ids = pltpu.make_async_copy(chosen, ids.at[g], local.at[0])
    own_grad = pltpu.make_async_copy(grad.at[:, columns(s, width)], group.at[s], local.at[1])
    own_ids.start()
    own_grad.start()
    for c in copies:
        c.wait()
    own_ids.wait()
    own_grad.wait()


def exchange(n_exp, n_seq, chosen, grad):
    rows, width = grad.shape[0], grad.shape[1] // n_seq
    dma = pltpu.SemaphoreType.DMA
    return pl.pallas_call(
        functools.partial(exchange_kernel, n_exp, n_seq),
        out_shape=(
            jax.ShapeDtypeStruct((n_exp,) + chosen.shape, chosen.dtype),
            jax.ShapeDtypeStruct((n_seq, rows, width), grad.dtype),
        ),
        in_specs=[VMEM, VMEM],
        out_specs=(VMEM, VMEM),
        scratch_shapes=[dma((n_exp,)), dma((n_exp,)), dma((n_seq,)), dma((n_seq,)), dma((2,))],
        compiler_params=pltpu.CompilerParams(collective_id=0, has_side_effects=True),
    )(chosen, grad)


def dispatch_kernel(n_exp, out, fetched, s0, r0, sa, ra, sb, rb, sc, rc, local):
    g, s = lax.axis_index("exp"), lax.axis_index("seq")
    width = out.shape[2]
    across, beside = (g, flip(s, 2)), (g, flip(s, 1))
    own, theirs = columns(s, width), columns(flip(s, 2), width)
    greet([(flip(g, k), s) for k in range(1, n_exp)] + [across, beside])
    first = pltpu.make_async_copy(out.at[g], fetched.at[g, :, own], local)
    first.start()
    half = n_exp // 2
    order = []
    for k in range(half):
        order.append(half + k)
        if k:
            order.append(k)
    sends = {}
    for k in order:
        e = flip(g, k)
        sends[k] = remote(out.at[e], fetched.at[g, :, own], s0.at[k], r0.at[k], (e, s))
        sends[k].start()
    crossed, done = [], []
    for k in range(n_exp):
        block = fetched.at[flip(g, k)]
        if k:
            sends[k].wait_recv()
        else:
            first.wait()
        c = remote(block.at[:, own], block.at[:, own], sa.at[k], ra.at[k], across)
        c.start()
        crossed.append(c)
        d = remote(block.at[:, own], block.at[:, own], sb.at[k], rb.at[k], beside)
        d.start()
        done.append(d)
    for k in range(n_exp):
        block = fetched.at[flip(g, k)]
        crossed[k].wait_recv()
        d = remote(block.at[:, theirs], block.at[:, theirs], sc.at[k], rc.at[k], beside)
        d.start()
        done.append(d)
    for k in order:
        sends[k].wait_send()
    for c in crossed:
        c.wait_send()
    for d in done:
        d.wait()


def dispatch(n_exp, n_seq, out):
    rows, width = out.shape[1:]
    dma = pltpu.SemaphoreType.DMA
    return pl.pallas_call(
        functools.partial(dispatch_kernel, n_exp),
        out_shape=jax.ShapeDtypeStruct((n_exp, rows, n_seq * width), out.dtype),
        in_specs=[ANY],
        out_specs=ANY,
        scratch_shapes=[dma((n_exp,))] * 8 + [dma],
        compiler_params=pltpu.CompilerParams(collective_id=1, has_side_effects=True),
    )(out)


def combine_kernel(n_exp, part, arrived, near, sum1, far, sum2, s1, r1, s2, r2, s3, r3, local):
    g, s = lax.axis_index("exp"), lax.axis_index("seq")
    width = arrived.shape[2]
    across, beside = (g, flip(s, 2)), (g, flip(s, 1))
    own, theirs = columns(s, width), columns(flip(s, 2), width)
    greet([(flip(g, k), s) for k in range(1, n_exp)] + [across, beside])
    half = n_exp // 2
    order = list(range(half, n_exp)) + list(range(1, half)) + [0]
    pairs = {}
    for k in order:
        e = flip(g, k)
        pairs[k] = [
            remote(
                part.at[e, :, columns(flip(s, bits), width)],
                near.at[e, i],
                s1.at[k, i],
                r1.at[k, i],
                beside,
            )
            for i, bits in enumerate((3, 1))
        ]
        for c in pairs[k]:
            c.start()
    middle, last = {}, {}
    for k in order:
        e = flip(g, k)
        pairs[k][0].wait_recv()
        both = part[e, :, theirs].astype(jnp.float32) + near[e, 0].astype(jnp.float32)
        sum1[e] = both.astype(jnp.bfloat16)
        middle[k] = remote(sum1.at[e], far.at[e], s2.at[k], r2.at[k], across)
        middle[k].start()
    for k in order:
        e = flip(g, k)
        pairs[k][1].wait_recv()
        middle[k].wait_recv()
        total = part[e, :, own].astype(jnp.float32) + near[e, 1].astype(jnp.float32)
        total = total + far[e].astype(jnp.float32)
        sum2[e] = total.astype(jnp.bfloat16)
        if k:
            last[k] = remote(sum2.at[e], arrived.at[g], s3.at[k], r3.at[k], (e, s))
        else:
            last[k] = pltpu.make_async_copy(sum2.at[e], arrived.at[g], local)
        last[k].start()
    for k in order:
        for c in pairs[k]:
            c.wait_send()
        middle[k].wait_send()
        last[k].wait()


def combine(n_exp, n_seq, part):
    rows, width = part.shape[1], part.shape[2] // n_seq
    dma = pltpu.SemaphoreType.DMA
    block = pltpu.VMEM((n_exp, rows, width), part.dtype)
    return pl.pallas_call(
        functools.partial(combine_kernel, n_exp),
        out_shape=jax.ShapeDtypeStruct((n_exp, rows, width), part.dtype),
        in_specs=[VMEM],
        out_specs=VMEM,
        scratch_shapes=[pltpu.VMEM((n_exp, 2, rows, width), part.dtype), block, block, block]
        + [dma((n_exp, 2))] * 2
        + [dma((n_exp,))] * 4
        + [dma],
        compiler_params=pltpu.CompilerParams(
            collective_id=2, has_side_effects=True, vmem_limit_bytes=48 * 2**20
        ),
    )(part)


def expert_kernel(
    n_exp, out, gate, up, weight, down, mixing, arrived, score,
    fetched, both, part, near, sum1, far, sum2,
    s0, r0, sa, ra, sb, rb, sc, rc, s1, r1, s2, r2, s3, r3, local,
):
    g, s = lax.axis_index("exp"), lax.axis_index("seq")
    width = out.shape[2]
    hidden_part = gate.shape[2]
    across, beside = (g, flip(s, 2)), (g, flip(s, 1))
    own, theirs = columns(s, width), columns(flip(s, 2), width)
    greet([(flip(g, k), s) for k in range(1, n_exp)] + [across, beside])
    half = n_exp // 2
    place = [flip(g, k) for k in range(n_exp)]
    first = pltpu.make_async_copy(out.at[g], fetched.at[g, :, own], local.at[0])
    first.start()
    sends, crossed, moved, turned, pairs, middle, last = {}, {}, {}, {}, {}, {}, {}

    def send(k):
        sends[k] = remote(
            out.at[place[k]], fetched.at[g, :, own], s0.at[k], r0.at[k], (place[k], s)
        )
        sends[k].start()

    def spread(k):
        block = fetched.at[place[k], :, own]
        if k:
            sends[k].wait_recv()
        else:
            first.wait()
        crossed[k] = remote(block, block, sa.at[k], ra.at[k], across)
        crossed[k].start()
        moved[k] = remote(block, block, sb.at[k], rb.at[k], beside)
        moved[k].start()

    def turn(k):
        block = fetched.at[place[k], :, theirs]
        crossed[k].wait_recv()
        turned[k] = remote(block, block, sc.at[k], rc.at[k], beside)
        turned[k].start()

    def compute(k):
        e = place[k]
        moved[k].wait_recv()
        turned[k].wait_recv()
        back = lax.dot_general(
            fetched[e], down[...], (((1,), (1,)), ((), ())), preferred_element_type=jnp.float32
        )
        gate_pre = gate[e].astype(jnp.float32)
        up_pre = up[e].astype(jnp.float32)
        sigmoid_gate = jax.nn.sigmoid(gate_pre)
        activated = gate_pre * sigmoid_gate
        hidden = (activated * up_pre).astype(jnp.bfloat16)
        score[e] = jnp.sum(hidden.astype(jnp.float32) * back, axis=1, keepdims=True)
        scaled = weight[e] * back
        d_gate = scaled * up_pre * sigmoid_gate * (1.0 + gate_pre * (1.0 - sigmoid_gate))
        both[:, :hidden_part] = d_gate.astype(jnp.bfloat16)
        both[:, hidden_part:] = (scaled * activated).astype(jnp.bfloat16)

        @pl.loop(0, mixing.shape[0] // 512)
        def _(i):
            tile = columns(i, 512)
            part[e, :, tile] = lax.dot_general(
                both[...],
                mixing[tile, :],
                (((1,), (1,)), ((), ())),
                preferred_element_type=jnp.float32,
            ).astype(jnp.bfloat16)

        pairs[k] = [
            remote(
                part.at[e, :, columns(flip(s, bits), width)],
                near.at[e, i],
                s1.at[k, i],
                r1.at[k, i],
                beside,
            )
            for i, bits in enumerate((3, 1))
        ]
        for c in pairs[k]:
            c.start()

    def hand(k):
        e = place[k]
        pairs[k][0].wait_recv()
        value = part[e, :, theirs].astype(jnp.float32) + near[e, 0].astype(jnp.float32)
        sum1[e] = value.astype(jnp.bfloat16)
        middle[k] = remote(sum1.at[e], far.at[e], s2.at[k], r2.at[k], across)
        middle[k].start()

    def give(k):
        e = place[k]
        pairs[k][1].wait_recv()
        middle[k].wait_recv()
        value = part[e, :, own].astype(jnp.float32) + near[e, 1].astype(jnp.float32)
        value = value + far[e].astype(jnp.float32)
        sum2[e] = value.astype(jnp.bfloat16)
        if k:
            last[k] = remote(sum2.at[e], arrived.at[g], s3.at[k], r3.at[k], (e, s))
        else:
            last[k] = pltpu.make_async_copy(sum2.at[e], arrived.at[g], local.at[1])
        last[k].start()

    batches = [list(range(half))] + [list(range(k, k + 2)) for k in range(half, n_exp, 2)]
    for k in batches[1]:
        send(k)
    for k in batches[0][1:]:
        send(k)
    previous = []
    for i, batch in enumerate(batches):
        for k in batch:
            spread(k)
        if 0 < i < len(batches) - 1:
            for k in batches[i + 1]:
                send(k)
        for k in previous:
            give(k)
        for k in batch:
            turn(k)
        for j, k in enumerate(batch):
            compute(k)
            if j:
                hand(batch[j - 1])
        hand(batch[-1])
        previous = batch
    for k in previous:
        give(k)
    for k in range(n_exp):
        if k:
            sends[k].wait_send()
        crossed[k].wait_send()
        moved[k].wait_send()
        turned[k].wait_send()
        for c in pairs[k]:
            c.wait_send()
        middle[k].wait_send()
        last[k].wait()


def expert(n_exp, n_seq, out, gate, up, weight, down, mixing):
    rows, width = out.shape[1:]
    model_width = n_seq * width
    dma = pltpu.SemaphoreType.DMA
    block = pltpu.VMEM((n_exp, rows, width), out.dtype)
    whole = pltpu.VMEM((n_exp, rows, model_width), out.dtype)
    return pl.pallas_call(
        functools.partial(expert_kernel, n_exp),
        out_shape=(
            jax.ShapeDtypeStruct((n_exp, rows, width), out.dtype),
            jax.ShapeDtypeStruct((n_exp, rows, 1), jnp.float32),
        ),
        in_specs=[VMEM] * 6,
        out_specs=(VMEM, VMEM),
        scratch_shapes=[whole, pltpu.VMEM((rows, mixing.shape[1]), out.dtype), whole]
        + [pltpu.VMEM((n_exp, 2, rows, width), out.dtype), block, block, block]
        + [dma((n_exp,))] * 8
        + [dma((n_exp, 2))] * 2
        + [dma((n_exp,))] * 4
        + [dma((2,))],
        compiler_params=pltpu.CompilerParams(
            collective_id=4, has_side_effects=True, vmem_limit_bytes=58 * 2**20
        ),
    )(out, gate, up, weight, down, mixing)


def regroup_kernel(
    n_seq, totals, score, out, score_sum, scores, send, recv, send_s, recv_s, local
):
    g, s = lax.axis_index("exp"), lax.axis_index("seq")
    width = totals.shape[2]
    own = columns(s, width)
    greet([(g, flip(s, k)) for k in range(1, n_seq)])
    copies = []
    for k in range(n_seq - 1, 0, -1):
        t = flip(s, k)
        copies.append(remote(totals.at[t], out.at[:, own], send.at[k], recv.at[k], (g, t)))
        copies[-1].start()
        copies.append(remote(score, scores.at[s], send_s.at[k], recv_s.at[k], (g, t)))
        copies[-1].start()
    mine = pltpu.make_async_copy(totals.at[s], out.at[:, own], local)
    mine.start()
    scores[s] = score[...]
    for c in copies:
        c.wait()
    value = scores[0]
    for k in range(1, n_seq):
        value = value + scores[k]
    score_sum[...] = value
    mine.wait()


def regroup(n_seq, totals, score):
    rows, width = totals.shape[1:]
    dma = pltpu.SemaphoreType.DMA
    return pl.pallas_call(
        functools.partial(regroup_kernel, n_seq),
        out_shape=(
            jax.ShapeDtypeStruct((rows, n_seq * width), totals.dtype),
            jax.ShapeDtypeStruct(score.shape, score.dtype),
        ),
        in_specs=[VMEM, VMEM],
        out_specs=(VMEM, VMEM),
        scratch_shapes=[pltpu.VMEM((n_seq,) + score.shape, score.dtype)]
        + [dma((n_seq,))] * 4
        + [dma],
        compiler_params=pltpu.CompilerParams(collective_id=3, has_side_effects=True),
    )(totals, score)


def local(out_grad, chosen, scores, saved_pre, gate_up, down):
    n_exp = lax.axis_size("exp")
    n_seq = lax.axis_size("seq")
    capacity = chosen.shape[1]
    slot_most = 9 * capacity // (8 * n_exp)
    tok_count, model_width = out_grad.shape
    width = model_width // n_seq
    group_tok = tok_count * n_seq
    pad_rows = n_exp * slot_most
    hidden_part = gate_up.shape[3]
    group_index = lax.axis_index("exp")

    own_ids = chosen[0]
    owner_group = own_ids // group_tok
    owner_hits = (owner_group[None, :] == jnp.arange(n_exp, dtype=jnp.int32)[:, None]).astype(
        jnp.int32
    )
    slot_order = jnp.sum(jnp.cumsum(owner_hits, axis=1) * owner_hits, axis=0) - 1
    position = owner_group * slot_most + slot_order
    place = position[None, :] == jnp.arange(pad_rows, dtype=jnp.int32)[:, None]
    weight_padded = jnp.sum(jnp.where(place, scores[0][None, :], 0.0), axis=1)
    place_one = place.astype(jnp.bfloat16)

    def padded(x):
        return jnp.dot(place_one, x, preferred_element_type=jnp.float32)

    gate_pre = padded(saved_pre[0, :, 0])
    up_pre = padded(saved_pre[0, :, 1])
    mixing = gate_up[0].reshape(model_width, 2 * hidden_part)

    ids, group = exchange(n_exp, n_seq, chosen.reshape(capacity // 128, 128), out_grad)
    local_ids = ids.reshape(n_exp, capacity) - group_index * group_tok
    inside = (local_ids >= 0) & (local_ids < group_tok)
    slot_rank = jnp.cumsum(inside.astype(jnp.int32), axis=1) - 1
    slot_ids = jnp.arange(slot_most, dtype=jnp.int32)
    picked = inside[:, None, :] & (slot_rank[:, None, :] == slot_ids[None, :, None])
    source = jnp.sum(jnp.where(picked, local_ids[:, None, :] + 1, 0), axis=2).reshape(pad_rows) - 1
    tokens = jnp.arange(group_tok, dtype=jnp.int32)
    take = (source[:, None] == tokens[None, :]).astype(jnp.bfloat16)
    outgoing = jnp.dot(
        take, group.reshape(group_tok, width), preferred_element_type=jnp.float32
    ).astype(jnp.bfloat16)
    outgoing = outgoing.reshape(n_exp, slot_most, width)
    if slot_most % 16 == 0:
        arrived, score_part = expert(
            n_exp,
            n_seq,
            outgoing,
            gate_pre.astype(jnp.bfloat16).reshape(n_exp, slot_most, hidden_part),
            up_pre.astype(jnp.bfloat16).reshape(n_exp, slot_most, hidden_part),
            weight_padded.reshape(n_exp, slot_most, 1),
            down[0],
            mixing,
        )
        score_part = score_part.reshape(pad_rows)
    else:
        fetched = dispatch(n_exp, n_seq, outgoing)
        fetched = fetched.reshape(pad_rows, model_width)

        back_grad = lax.dot_general(
            fetched, down[0], (((1,), (1,)), ((), ())), preferred_element_type=jnp.float32
        )
        sigmoid_gate = jax.nn.sigmoid(gate_pre)
        activated = gate_pre * sigmoid_gate
        hidden = (activated * up_pre).astype(jnp.bfloat16)
        hidden = lax.optimization_barrier(hidden)
        score_part = jnp.sum(hidden.astype(jnp.float32) * back_grad, axis=1)
        scaled = weight_padded[:, None] * back_grad
        d_gate = scaled * up_pre * sigmoid_gate * (1.0 + gate_pre * (1.0 - sigmoid_gate))
        d_up = scaled * activated
        d_both = jnp.concatenate([d_gate, d_up], axis=1).astype(jnp.bfloat16)
        partial_value = lax.dot_general(
            d_both, mixing, (((1,), (1,)), ((), ())), preferred_element_type=jnp.float32
        ).astype(jnp.bfloat16)
        arrived = combine(n_exp, n_seq, partial_value.reshape(n_exp, slot_most, model_width))
    score_slots = jnp.sum(jnp.where(place, score_part[:, None], 0.0), axis=0)
    totals = lax.dot_general(
        take,
        arrived.reshape(pad_rows, width),
        (((0,), (0,)), ((), ())),
        preferred_element_type=jnp.float32,
    ).astype(jnp.bfloat16)
    summed, score_grad = regroup(
        n_seq,
        totals.reshape(n_seq, tok_count, width),
        score_slots.reshape(capacity // 128, 128),
    )
    return (summed, score_grad.reshape(1, capacity))


def solution(mesh):
    return jax.shard_map(
        local,
        mesh=mesh,
        in_specs=(
            P(("exp", "seq"), None),
            P("exp", None),
            P("exp", None),
            P("exp", None, None, "seq"),
            P("exp", None, None, "seq"),
            P("exp", "seq", None),
        ),
        out_specs=(P(("exp", "seq"), None), P("exp", None)),
        check_vma=False,
    )
```

```python
import functools

import jax
import jax.numpy as jnp
from jax import lax
from jax.experimental import pallas as pl
from jax.experimental.pallas import tpu as pltpu
from jax.sharding import PartitionSpec as P

MESH = pl.DeviceIdType.MESH
ANY = pl.BlockSpec(memory_space=pl.ANY)
VMEM = pl.BlockSpec(memory_space=pltpu.VMEM)


def flip(index, bits):
    out, step = index, 1
    while bits >= step:
        if bits & step:
            out = out + step * (1 - 2 * ((index // step) % 2))
        step *= 2
    return out


def greet(peers):
    barrier = pltpu.get_barrier_semaphore()
    for p in peers:
        pl.semaphore_signal(barrier, inc=1, device_id=p, device_id_type=MESH)
    pl.semaphore_wait(barrier, len(peers))


def remote(src, dst, send, recv, to):
    return pltpu.make_async_remote_copy(
        src_ref=src, dst_ref=dst, send_sem=send, recv_sem=recv, device_id=to, device_id_type=MESH
    )


def columns(quarter, width):
    return pl.ds(pl.multiple_of(quarter * width, 128), width)


def exchange_kernel(n_exp, n_seq, chosen, grad, ids, group, send_i, recv_i, send_g, recv_g, local):
    g, s = lax.axis_index("exp"), lax.axis_index("seq")
    width = grad.shape[1] // n_seq
    greet([(flip(g, k), s) for k in range(1, n_exp)] + [(g, flip(s, k)) for k in range(1, n_seq)])
    copies = []
    for k in range(1, n_exp):
        copies.append(remote(chosen, ids.at[g], send_i.at[k], recv_i.at[k], (flip(g, k), s)))
        copies[-1].start()
    for k in range(n_seq - 1, 0, -1):
        t = flip(s, k)
        copies.append(
            remote(grad.at[:, columns(t, width)], group.at[s], send_g.at[k], recv_g.at[k], (g, t))
        )
        copies[-1].start()
    own_ids = pltpu.make_async_copy(chosen, ids.at[g], local.at[0])
    own_grad = pltpu.make_async_copy(grad.at[:, columns(s, width)], group.at[s], local.at[1])
    own_ids.start()
    own_grad.start()
    for c in copies:
        c.wait()
    own_ids.wait()
    own_grad.wait()


def exchange(n_exp, n_seq, chosen, grad):
    rows, width = grad.shape[0], grad.shape[1] // n_seq
    dma = pltpu.SemaphoreType.DMA
    return pl.pallas_call(
        functools.partial(exchange_kernel, n_exp, n_seq),
        out_shape=(
            jax.ShapeDtypeStruct((n_exp,) + chosen.shape, chosen.dtype),
            jax.ShapeDtypeStruct((n_seq, rows, width), grad.dtype),
        ),
        in_specs=[VMEM, VMEM],
        out_specs=(VMEM, VMEM),
        scratch_shapes=[dma((n_exp,)), dma((n_exp,)), dma((n_seq,)), dma((n_seq,)), dma((2,))],
        compiler_params=pltpu.CompilerParams(collective_id=0, has_side_effects=True),
    )(chosen, grad)


def dispatch_kernel(n_exp, out, fetched, s0, r0, sa, ra, sb, rb, sc, rc, local):
    g, s = lax.axis_index("exp"), lax.axis_index("seq")
    width = out.shape[2]
    across, beside = (g, flip(s, 2)), (g, flip(s, 1))
    own, theirs = columns(s, width), columns(flip(s, 2), width)
    greet([(flip(g, k), s) for k in range(1, n_exp)] + [across, beside])
    first = pltpu.make_async_copy(out.at[g], fetched.at[g, :, own], local)
    first.start()
    half = n_exp // 2
    order = []
    for k in range(half):
        order.append(half + k)
        if k:
            order.append(k)
    sends = {}
    for k in order:
        e = flip(g, k)
        sends[k] = remote(out.at[e], fetched.at[g, :, own], s0.at[k], r0.at[k], (e, s))
        sends[k].start()
    crossed, done = [], []
    for k in range(n_exp):
        block = fetched.at[flip(g, k)]
        if k:
            sends[k].wait_recv()
        else:
            first.wait()
        c = remote(block.at[:, own], block.at[:, own], sa.at[k], ra.at[k], across)
        c.start()
        crossed.append(c)
        d = remote(block.at[:, own], block.at[:, own], sb.at[k], rb.at[k], beside)
        d.start()
        done.append(d)
    for k in range(n_exp):
        block = fetched.at[flip(g, k)]
        crossed[k].wait_recv()
        d = remote(block.at[:, theirs], block.at[:, theirs], sc.at[k], rc.at[k], beside)
        d.start()
        done.append(d)
    for k in order:
        sends[k].wait_send()
    for c in crossed:
        c.wait_send()
    for d in done:
        d.wait()


def dispatch(n_exp, n_seq, out):
    rows, width = out.shape[1:]
    dma = pltpu.SemaphoreType.DMA
    return pl.pallas_call(
        functools.partial(dispatch_kernel, n_exp),
        out_shape=jax.ShapeDtypeStruct((n_exp, rows, n_seq * width), out.dtype),
        in_specs=[ANY],
        out_specs=ANY,
        scratch_shapes=[dma((n_exp,))] * 8 + [dma],
        compiler_params=pltpu.CompilerParams(collective_id=1, has_side_effects=True),
    )(out)


def combine_kernel(n_exp, part, arrived, near, sum1, far, sum2, s1, r1, s2, r2, s3, r3, local):
    g, s = lax.axis_index("exp"), lax.axis_index("seq")
    width = arrived.shape[2]
    across, beside = (g, flip(s, 2)), (g, flip(s, 1))
    own, theirs = columns(s, width), columns(flip(s, 2), width)
    greet([(flip(g, k), s) for k in range(1, n_exp)] + [across, beside])
    half = n_exp // 2
    order = list(range(half, n_exp)) + list(range(1, half)) + [0]
    pairs = {}
    for k in order:
        e = flip(g, k)
        pairs[k] = [
            remote(
                part.at[e, :, columns(flip(s, bits), width)],
                near.at[e, i],
                s1.at[k, i],
                r1.at[k, i],
                beside,
            )
            for i, bits in enumerate((3, 1))
        ]
        for c in pairs[k]:
            c.start()
    middle, last = {}, {}
    for k in order:
        e = flip(g, k)
        pairs[k][0].wait_recv()
        both = part[e, :, theirs].astype(jnp.float32) + near[e, 0].astype(jnp.float32)
        sum1[e] = both.astype(jnp.bfloat16)
        middle[k] = remote(sum1.at[e], far.at[e], s2.at[k], r2.at[k], across)
        middle[k].start()
    for k in order:
        e = flip(g, k)
        pairs[k][1].wait_recv()
        middle[k].wait_recv()
        total = part[e, :, own].astype(jnp.float32) + near[e, 1].astype(jnp.float32)
        total = total + far[e].astype(jnp.float32)
        sum2[e] = total.astype(jnp.bfloat16)
        if k:
            last[k] = remote(sum2.at[e], arrived.at[g], s3.at[k], r3.at[k], (e, s))
        else:
            last[k] = pltpu.make_async_copy(sum2.at[e], arrived.at[g], local)
        last[k].start()
    for k in order:
        for c in pairs[k]:
            c.wait_send()
        middle[k].wait_send()
        last[k].wait()


def combine(n_exp, n_seq, part):
    rows, width = part.shape[1], part.shape[2] // n_seq
    dma = pltpu.SemaphoreType.DMA
    block = pltpu.VMEM((n_exp, rows, width), part.dtype)
    return pl.pallas_call(
        functools.partial(combine_kernel, n_exp),
        out_shape=jax.ShapeDtypeStruct((n_exp, rows, width), part.dtype),
        in_specs=[VMEM],
        out_specs=VMEM,
        scratch_shapes=[pltpu.VMEM((n_exp, 2, rows, width), part.dtype), block, block, block]
        + [dma((n_exp, 2))] * 2
        + [dma((n_exp,))] * 4
        + [dma],
        compiler_params=pltpu.CompilerParams(
            collective_id=2, has_side_effects=True, vmem_limit_bytes=48 * 2**20
        ),
    )(part)


def plan(n_exp):
    half = n_exp // 2
    near = list(range(half))
    order = [("send", k) for k in range(1, half + 2)]
    order += [("spread", 0), ("spread", 1), ("turn", 0), ("compute", 0)]
    order += [("spread", k) for k in near[2:]] + [("send", k) for k in range(half + 2, n_exp)]
    order += [("turn", 1), ("compute", 1), ("hand", 0)] + [("turn", k) for k in near[2:]]
    for k in near[2:]:
        order += [("compute", k), ("hand", k - 1)]
    order += [("hand", half - 1)]
    before = near
    for i in range(half, n_exp, 2):
        j = i + 1
        order += [("spread", i), ("spread", j)] + [("give", k) for k in before]
        order += [("turn", i), ("turn", j), ("compute", i)]
        if j < n_exp - 1:
            order += [("compute", j), ("hand", i), ("hand", j)]
        else:
            order += [("hand", i), ("compute", j), ("hand", j)]
        before = [i, j]
    return order + [("give", k) for k in before]


def expert_kernel(
    n_exp, out, gate, up, weight, down, mixing, arrived, score,
    fetched, both, part, near, sum1, far, sum2,
    s0, r0, sa, ra, sb, rb, sc, rc, s1, r1, s2, r2, s3, r3, local,
):
    g, s = lax.axis_index("exp"), lax.axis_index("seq")
    width = out.shape[2]
    hidden_part = gate.shape[2]
    across, beside = (g, flip(s, 2)), (g, flip(s, 1))
    own, theirs = columns(s, width), columns(flip(s, 2), width)
    greet([(flip(g, k), s) for k in range(1, n_exp)] + [across, beside])
    place = [flip(g, k) for k in range(n_exp)]
    first = pltpu.make_async_copy(out.at[g], fetched.at[g, :, own], local.at[0])
    first.start()
    sends, crossed, moved, turned, pairs, middle, last = {}, {}, {}, {}, {}, {}, {}

    def send(k):
        sends[k] = remote(
            out.at[place[k]], fetched.at[g, :, own], s0.at[k], r0.at[k], (place[k], s)
        )
        sends[k].start()

    def spread(k):
        block = fetched.at[place[k], :, own]
        if k:
            sends[k].wait_recv()
        else:
            first.wait()
        crossed[k] = remote(block, block, sa.at[k], ra.at[k], across)
        crossed[k].start()
        moved[k] = remote(block, block, sb.at[k], rb.at[k], beside)
        moved[k].start()

    def turn(k):
        block = fetched.at[place[k], :, theirs]
        crossed[k].wait_recv()
        turned[k] = remote(block, block, sc.at[k], rc.at[k], beside)
        turned[k].start()

    def compute(k):
        e = place[k]
        moved[k].wait_recv()
        turned[k].wait_recv()
        back = lax.dot_general(
            fetched[e], down[...], (((1,), (1,)), ((), ())), preferred_element_type=jnp.float32
        )
        gate_pre = gate[e].astype(jnp.float32)
        up_pre = up[e].astype(jnp.float32)
        sigmoid_gate = jax.nn.sigmoid(gate_pre)
        activated = gate_pre * sigmoid_gate
        hidden = (activated * up_pre).astype(jnp.bfloat16)
        score[e] = jnp.sum(hidden.astype(jnp.float32) * back, axis=1, keepdims=True)
        scaled = weight[e] * back
        d_gate = scaled * up_pre * sigmoid_gate * (1.0 + gate_pre * (1.0 - sigmoid_gate))
        both[:, :hidden_part] = d_gate.astype(jnp.bfloat16)
        both[:, hidden_part:] = (scaled * activated).astype(jnp.bfloat16)

        @pl.loop(0, mixing.shape[0] // 512)
        def _(i):
            tile = columns(i, 512)
            part[e, :, tile] = lax.dot_general(
                both[...],
                mixing[tile, :],
                (((1,), (1,)), ((), ())),
                preferred_element_type=jnp.float32,
            ).astype(jnp.bfloat16)

        pairs[k] = [
            remote(
                part.at[e, :, columns(flip(s, bits), width)],
                near.at[e, i],
                s1.at[k, i],
                r1.at[k, i],
                beside,
            )
            for i, bits in enumerate((3, 1))
        ]
        for c in pairs[k]:
            c.start()

    def hand(k):
        e = place[k]
        pairs[k][0].wait_recv()
        value = part[e, :, theirs].astype(jnp.float32) + near[e, 0].astype(jnp.float32)
        sum1[e] = value.astype(jnp.bfloat16)
        middle[k] = remote(sum1.at[e], far.at[e], s2.at[k], r2.at[k], across)
        middle[k].start()

    def give(k):
        e = place[k]
        pairs[k][1].wait_recv()
        middle[k].wait_recv()
        value = part[e, :, own].astype(jnp.float32) + near[e, 1].astype(jnp.float32)
        value = value + far[e].astype(jnp.float32)
        sum2[e] = value.astype(jnp.bfloat16)
        if k:
            last[k] = remote(sum2.at[e], arrived.at[g], s3.at[k], r3.at[k], (e, s))
        else:
            last[k] = pltpu.make_async_copy(sum2.at[e], arrived.at[g], local.at[1])
        last[k].start()

    steps = {"send": send, "spread": spread, "turn": turn}
    steps.update({"compute": compute, "hand": hand, "give": give})
    for step, k in plan(n_exp):
        steps[step](k)
    for k in range(n_exp):
        if k:
            sends[k].wait_send()
        crossed[k].wait_send()
        moved[k].wait_send()
        turned[k].wait_send()
        for c in pairs[k]:
            c.wait_send()
        middle[k].wait_send()
        last[k].wait()


def expert(n_exp, n_seq, out, gate, up, weight, down, mixing):
    rows, width = out.shape[1:]
    model_width = n_seq * width
    dma = pltpu.SemaphoreType.DMA
    block = pltpu.VMEM((n_exp, rows, width), out.dtype)
    whole = pltpu.VMEM((n_exp, rows, model_width), out.dtype)
    return pl.pallas_call(
        functools.partial(expert_kernel, n_exp),
        out_shape=(
            jax.ShapeDtypeStruct((n_exp, rows, width), out.dtype),
            jax.ShapeDtypeStruct((n_exp, rows, 1), jnp.float32),
        ),
        in_specs=[VMEM] * 6,
        out_specs=(VMEM, VMEM),
        scratch_shapes=[whole, pltpu.VMEM((rows, mixing.shape[1]), out.dtype), whole]
        + [pltpu.VMEM((n_exp, 2, rows, width), out.dtype), block, block, block]
        + [dma((n_exp,))] * 8
        + [dma((n_exp, 2))] * 2
        + [dma((n_exp,))] * 4
        + [dma((2,))],
        compiler_params=pltpu.CompilerParams(
            collective_id=4, has_side_effects=True, vmem_limit_bytes=58 * 2**20
        ),
    )(out, gate, up, weight, down, mixing)


def regroup_kernel(
    n_seq, totals, score, out, score_sum, scores, send, recv, send_s, recv_s, local
):
    g, s = lax.axis_index("exp"), lax.axis_index("seq")
    width = totals.shape[2]
    own = columns(s, width)
    greet([(g, flip(s, k)) for k in range(1, n_seq)])
    copies = []
    for k in range(n_seq - 1, 0, -1):
        t = flip(s, k)
        copies.append(remote(totals.at[t], out.at[:, own], send.at[k], recv.at[k], (g, t)))
        copies[-1].start()
        copies.append(remote(score, scores.at[s], send_s.at[k], recv_s.at[k], (g, t)))
        copies[-1].start()
    mine = pltpu.make_async_copy(totals.at[s], out.at[:, own], local)
    mine.start()
    scores[s] = score[...]
    for c in copies:
        c.wait()
    value = scores[0]
    for k in range(1, n_seq):
        value = value + scores[k]
    score_sum[...] = value
    mine.wait()


def regroup(n_seq, totals, score):
    rows, width = totals.shape[1:]
    dma = pltpu.SemaphoreType.DMA
    return pl.pallas_call(
        functools.partial(regroup_kernel, n_seq),
        out_shape=(
            jax.ShapeDtypeStruct((rows, n_seq * width), totals.dtype),
            jax.ShapeDtypeStruct(score.shape, score.dtype),
        ),
        in_specs=[VMEM, VMEM],
        out_specs=(VMEM, VMEM),
        scratch_shapes=[pltpu.VMEM((n_seq,) + score.shape, score.dtype)]
        + [dma((n_seq,))] * 4
        + [dma],
        compiler_params=pltpu.CompilerParams(collective_id=3, has_side_effects=True),
    )(totals, score)


def local(out_grad, chosen, scores, saved_pre, gate_up, down):
    n_exp = lax.axis_size("exp")
    n_seq = lax.axis_size("seq")
    capacity = chosen.shape[1]
    slot_most = 9 * capacity // (8 * n_exp)
    tok_count, model_width = out_grad.shape
    width = model_width // n_seq
    group_tok = tok_count * n_seq
    pad_rows = n_exp * slot_most
    hidden_part = gate_up.shape[3]
    group_index = lax.axis_index("exp")

    own_ids = chosen[0]
    owner_group = own_ids // group_tok
    owner_hits = (owner_group[None, :] == jnp.arange(n_exp, dtype=jnp.int32)[:, None]).astype(
        jnp.int32
    )
    slot_order = jnp.sum(jnp.cumsum(owner_hits, axis=1) * owner_hits, axis=0) - 1
    position = owner_group * slot_most + slot_order
    place = position[None, :] == jnp.arange(pad_rows, dtype=jnp.int32)[:, None]
    weight_padded = jnp.sum(jnp.where(place, scores[0][None, :], 0.0), axis=1)
    place_one = place.astype(jnp.bfloat16)

    def padded(x):
        return jnp.dot(place_one, x, preferred_element_type=jnp.float32)

    gate_pre = padded(saved_pre[0, :, 0])
    up_pre = padded(saved_pre[0, :, 1])
    mixing = gate_up[0].reshape(model_width, 2 * hidden_part)

    ids, group = exchange(n_exp, n_seq, chosen.reshape(capacity // 128, 128), out_grad)
    local_ids = ids.reshape(n_exp, capacity) - group_index * group_tok
    inside = (local_ids >= 0) & (local_ids < group_tok)
    slot_rank = jnp.cumsum(inside.astype(jnp.int32), axis=1) - 1
    slot_ids = jnp.arange(slot_most, dtype=jnp.int32)
    picked = inside[:, None, :] & (slot_rank[:, None, :] == slot_ids[None, :, None])
    source = jnp.sum(jnp.where(picked, local_ids[:, None, :] + 1, 0), axis=2).reshape(pad_rows) - 1
    tokens = jnp.arange(group_tok, dtype=jnp.int32)
    take = (source[:, None] == tokens[None, :]).astype(jnp.bfloat16)
    outgoing = jnp.dot(
        take, group.reshape(group_tok, width), preferred_element_type=jnp.float32
    ).astype(jnp.bfloat16)
    outgoing = outgoing.reshape(n_exp, slot_most, width)
    if slot_most % 16 == 0 and n_exp >= 4:
        arrived, score_part = expert(
            n_exp,
            n_seq,
            outgoing,
            gate_pre.astype(jnp.bfloat16).reshape(n_exp, slot_most, hidden_part),
            up_pre.astype(jnp.bfloat16).reshape(n_exp, slot_most, hidden_part),
            weight_padded.reshape(n_exp, slot_most, 1),
            down[0],
            mixing,
        )
        score_part = score_part.reshape(pad_rows)
    else:
        fetched = dispatch(n_exp, n_seq, outgoing)
        fetched = fetched.reshape(pad_rows, model_width)

        back_grad = lax.dot_general(
            fetched, down[0], (((1,), (1,)), ((), ())), preferred_element_type=jnp.float32
        )
        sigmoid_gate = jax.nn.sigmoid(gate_pre)
        activated = gate_pre * sigmoid_gate
        hidden = (activated * up_pre).astype(jnp.bfloat16)
        hidden = lax.optimization_barrier(hidden)
        score_part = jnp.sum(hidden.astype(jnp.float32) * back_grad, axis=1)
        scaled = weight_padded[:, None] * back_grad
        d_gate = scaled * up_pre * sigmoid_gate * (1.0 + gate_pre * (1.0 - sigmoid_gate))
        d_up = scaled * activated
        d_both = jnp.concatenate([d_gate, d_up], axis=1).astype(jnp.bfloat16)
        partial_value = lax.dot_general(
            d_both, mixing, (((1,), (1,)), ((), ())), preferred_element_type=jnp.float32
        ).astype(jnp.bfloat16)
        arrived = combine(n_exp, n_seq, partial_value.reshape(n_exp, slot_most, model_width))
    score_slots = jnp.sum(jnp.where(place, score_part[:, None], 0.0), axis=0)
    totals = lax.dot_general(
        take,
        arrived.reshape(pad_rows, width),
        (((0,), (0,)), ((), ())),
        preferred_element_type=jnp.float32,
    ).astype(jnp.bfloat16)
    summed, score_grad = regroup(
        n_seq,
        totals.reshape(n_seq, tok_count, width),
        score_slots.reshape(capacity // 128, 128),
    )
    return (summed, score_grad.reshape(1, capacity))


def solution(mesh):
    return jax.shard_map(
        local,
        mesh=mesh,
        in_specs=(
            P(("exp", "seq"), None),
            P("exp", None),
            P("exp", None),
            P("exp", None, None, "seq"),
            P("exp", None, None, "seq"),
            P("exp", "seq", None),
        ),
        out_specs=(P(("exp", "seq"), None), P("exp", None)),
        check_vma=False,
    )
```
